256 devices in a mesh: cube: 64 (over z, y, core), pair: 4 (over x).
Axes of the slice: x: 4, y: 4, z: 8, core: 2. Of those that a mesh axis runs over, the one named last changes fastest.
Arguments:
- own_partial: float32 [3, 16384, 512], P(None, 'cube'), may hold values from -6 to 6
- spill_partial: float32 [3, 16384, 512], P(None, 'cube'), may hold values from -6 to 6
- spill_box: int32 [16384], P('cube'), may hold values from 0 to 255, as said below
- sources: int32 [16384, 189], P('cube'), may hold values from 0 to 16383, as said below
- reflections: int32 [16384, 189], P('cube'), may hold values from 0 to 15
- operators: bfloat16 [16, 512, 512], P('pair'), may hold values from -0.01953125 to 0.01953125
Outputs:
- local_own: float32 [3, 16384, 512], P(None, 'cube', 'pair')
- local_spill: float32 [3, 16384, 512], P(None, 'cube', 'pair')
The draws below stay inside these ranges and needn't reach their ends.
Inputs may be any that keep to these rules, and one draw needn't show every extreme that they name: The sources of box b lie on b's owner or on the owner just before or after it: from max(0, (b // 256 - 1) * 256) to min(16384, (b // 256 + 2) * 256) - 1. A source may repeat within a list. `spill_box`: the 64 entries of each aligned run of 64 are distinct.
All inputs are finite; a program needn't handle non-finite values.
Results may differ from the reference program's by a relative error of at most 0.0095.
Values may be sent and summed in bfloat16 or wider, within the bound.
No kernel may reach another device: no remote copies, remote signals or barrier semaphores. Data moves between devices by JAX's collectives and lax.ppermute only.
A program may use at most 64 MiB of HBM per device.

```python
import jax
import jax.numpy as jnp
from jax import lax

E = 512
LIST = 189
REFL = 16
SPILL = 2
BOX_DEV = 256
CAPS = 64
SPILL_SLOTS = 256
SPILL_ALL = 16384
BOXES = 16384


def draw_spill_box(key, part):
    run_count = SPILL_ALL // CAPS
    scores = jax.random.randint(key, (run_count, BOX_DEV), 0, 1 << 20, dtype=jnp.int32)
    scores = scores * BOX_DEV + jnp.arange(BOX_DEV, dtype=jnp.int32)[None, :]
    ordering = jnp.argsort(scores, axis=1)
    return ordering[:, :CAPS].reshape(SPILL_ALL).astype(jnp.int32)


def draw_sources(key, part):
    owner_ids = jnp.arange(BOXES, dtype=jnp.int32) // BOX_DEV
    lowest = jnp.maximum(0, (owner_ids - 1) * BOX_DEV)
    highest = jnp.minimum(BOXES, (owner_ids + 2) * BOX_DEV)
    return jax.random.randint(key, (BOXES, LIST), lowest[:, None], highest[:, None], dtype=jnp.int32)


def set_ends(drawn, rng, least, largest):
    shape = drawn.shape
    place = [jax.random.randint(jax.random.fold_in(rng, axis), (), 0, shape[axis]) for axis in range(len(shape))]
    drawn = drawn.at[tuple(place)].set(least)
    longest = shape.index(max(shape))
    place[longest] = (place[longest] + 1) % shape[longest]
    return drawn.at[tuple(place)].set(largest)


def levels(rng, extent, pieces, least, high):
    loudness, own = 1.0, jax.random.fold_in(rng, 6)
    for position, blocks in pieces:
        steps = jnp.exp(jax.random.uniform(jax.random.fold_in(own, position), (blocks,), jnp.float32, least / len(pieces), high / len(pieces)))
        loudness = loudness * jnp.repeat(steps, extent[position] // blocks).reshape([-1 if axis == position else 1 for axis in range(len(extent))])
    return loudness


def bell_draw(own_key, extent, scale, most, cuts=(), kind=jnp.bfloat16):
    result = scale * jax.random.normal(own_key, extent, jnp.float32)
    if cuts:
        result = result * levels(own_key, extent, cuts, -0.22, 0.18)
    return jnp.clip(result, -most, most).astype(kind)


def setup_inputs(seed: int = 0) -> dict:
    streams_of = jax.random.split(jax.random.key(seed), 7)
    return {
        "own_partial": bell_draw(streams_of[0], (3, BOXES, E), 1.0, 6.0, ((1, 64),), jnp.float32),
        "spill_partial": bell_draw(streams_of[1], (3, SPILL_ALL, E), 1.0, 6.0, ((1, 64),), jnp.float32),
        "spill_box": draw_spill_box(jax.random.fold_in(streams_of[6], 71), 0),
        "sources": draw_sources(jax.random.fold_in(streams_of[6], 71), 0),
        "reflections": set_ends(jax.random.randint(streams_of[4], (BOXES, LIST), 0, REFL), jax.random.fold_in(streams_of[4], 1), 0, REFL - 1).astype(jnp.int32),
        "operators": bell_draw(streams_of[5], (REFL, E, E), (E * LIST) ** -0.5, 0.01953125, ((0, 4),)),
    }


def slot_targets():
    owner_count = BOXES // BOX_DEV
    slot_ids = jnp.arange(SPILL_ALL, dtype=jnp.int32)
    device_ids = slot_ids // SPILL_SLOTS
    group_ids = (slot_ids % SPILL_SLOTS) // CAPS
    offsets = jnp.where(group_ids < SPILL, group_ids - SPILL, group_ids - SPILL + 1)
    owners = device_ids + offsets
    valid = (owners >= 0) & (owners < owner_count)
    return owners, valid


def reference(own_partial, spill_partial, spill_box, sources, reflections, operators):
    owners, valid = slot_targets()
    slot_box = jnp.where(valid, owners * BOX_DEV + spill_box, BOXES).astype(jnp.int32)
    spill_rows = jnp.moveaxis(spill_partial, 1, 0)
    added = jax.ops.segment_sum(spill_rows, slot_box, num_segments=BOXES + 1)[:BOXES]
    multipole = (own_partial + jnp.moveaxis(added, 0, 1)).astype(jnp.bfloat16)
    refl_ids = jnp.arange(REFL, dtype=jnp.int32)[:, None]
    comp_ids = jnp.arange(3, dtype=jnp.int32)[None, :]
    sign_table = (1 - 2 * (jnp.right_shift(refl_ids, comp_ids) & 1)).astype(jnp.float32)
    transformed = jnp.einsum("cbe,ref->rcbf", multipole.astype(jnp.float32), operators.astype(jnp.float32),
                             precision=lax.Precision.HIGHEST)
    transformed = transformed * sign_table[:, :, None, None]
    blocks = BOXES // BOX_DEV
    src_blocks = sources.reshape(blocks, BOX_DEV, LIST)
    refl_blocks = reflections.reshape(blocks, BOX_DEV, LIST)

    def one_block(pair_in):
        src_part, refl_part = pair_in
        picked = transformed[refl_part, :, src_part, :]
        return jnp.sum(picked, axis=1)

    summed = lax.map(one_block, (src_blocks, refl_blocks))
    local_own = jnp.moveaxis(summed.reshape(BOXES, 3, E), 0, 1)
    safe_box = jnp.minimum(slot_box, BOXES - 1).astype(jnp.int32)
    local_spill = jnp.where(valid[None, :, None], local_own[:, safe_box, :], jnp.float32(0.0))
    return local_own, local_spill
```

```python
import jax
import jax.numpy as jnp
from jax import lax
from jax.experimental import pallas as pl
from jax.experimental.pallas import tpu as pltpu
from jax.sharding import PartitionSpec as P

BOX = 256
CAPS = 64
E = 512
COLS = 128
REFL = 16
SLOTS = 3 * REFL
MSG = 3 * CAPS + 16
BF = jnp.bfloat16
F32 = jnp.float32
ANY = pl.BlockSpec(memory_space=pl.ANY)
SMEM = pl.BlockSpec(memory_space=pltpu.SMEM)
VMEM = pl.BlockSpec(memory_space=pltpu.VMEM)


def params(mib=48):
    return pltpu.CompilerParams(vmem_limit_bytes=mib << 20)


def cost(flops, nbytes):
    return pl.CostEstimate(flops=int(flops), bytes_accessed=int(nbytes), transcendentals=0)


def swapped(value, pairs, count):
    target = list(range(count))
    for a, b in pairs:
        target[a], target[b] = b, a
    return lax.ppermute(value, "cube", list(enumerate(target)))


def neighbours(count):
    same = [(i, i + 1) for i in range(0, count, 2)]
    across = [(i, i + 1) for i in range(1, count - 1, 2)]
    even = [(i + c, i + 2 + c) for i in range(0, count - 2, 4) for c in (0, 1)]
    odd = [(i + c, i + 2 + c) for i in range(2, count - 2, 4) for c in (0, 1)]
    return same, across, even, odd


def pack_kernel(meta, spill, labels, *outs):
    for m, out in enumerate(outs):
        group = meta[m]
        rows = pl.ds(pl.multiple_of(group * CAPS, CAPS), CAPS)
        for c in range(3):
            out[c * CAPS : (c + 1) * CAPS, :] = spill[c, rows, :].astype(BF)
        out[3 * CAPS :, :] = jnp.broadcast_to(labels[pl.ds(group, 1), :], (16, E)).astype(BF)


def pack(meta, spill, labels):
    return pl.pallas_call(
        pack_kernel,
        in_specs=[SMEM, VMEM, VMEM],
        out_specs=[VMEM] * 4,
        out_shape=[jax.ShapeDtypeStruct((MSG, E), BF)] * 4,
        compiler_params=params(),
        cost_estimate=cost(1e6, 2.4e6),
        name="pack",
    )(meta, spill, labels)


TB = 32
TG = 16


def table_kernel(hi_ref, lo_ref, *rest):
    out_ref = rest[-1]
    hi_ids = lax.broadcasted_iota(jnp.int32, (SLOTS, 256), 0).astype(BF)
    lo_ids = lax.broadcasted_iota(jnp.int32, (BOX, 256), 0).astype(BF)
    one, zero = jnp.ones((), BF), jnp.zeros((), BF)
    for g in range(TB // TG):
        found = []
        for u in range(TG):
            t = g * TG + u
            high = jnp.where(hi_ids == hi_ref[t : t + 1, :].astype(BF), one, zero)
            low = jnp.where(lo_ids == lo_ref[t : t + 1, :].astype(BF), one, zero)
            found.append(
                lax.dot_general(
                    high, low, (((1,), (1,)), ((), ())), preferred_element_type=F32
                )
            )
        stacked = jnp.transpose(jnp.stack(found, 0), (1, 0, 2))
        out_ref[:, g * TG : (g + 1) * TG, :] = stacked.astype(BF)


def table(hi, lo, first, steps, into=None):
    extra = [] if into is None else [into]
    return pl.pallas_call(
        table_kernel,
        grid=(steps,),
        in_specs=[pl.BlockSpec((TB, 256), lambda i: (i + first, 0))] * 2 + [ANY] * len(extra),
        out_specs=pl.BlockSpec((SLOTS, TB, BOX), lambda i: (0, i + first, 0)),
        out_shape=jax.ShapeDtypeStruct((SLOTS, BOX, BOX), BF),
        input_output_aliases={2: 0} if extra else {},
        compiler_params=params(),
        cost_estimate=cost(steps * 1.2e9, 1e6 * steps),
        name="table",
    )(hi, lo, *extra)


def gather_kernel(own, *refs):
    messages, out, pick = refs[:4], refs[4], refs[5]
    lane = lax.broadcasted_iota(jnp.int32, (1, 256), 1) // CAPS
    label = jnp.zeros((1, 256), F32)
    for m, msg in enumerate(messages):
        label = jnp.where(lane == m, msg[3 * CAPS :, :256].astype(F32)[:1], label)
    boxes = lax.broadcasted_iota(jnp.int32, (BOX, 256), 0).astype(F32)
    picker = jnp.where(boxes == label, 1.0, 0.0).astype(BF)
    pick[...] = picker
    for c in range(3):
        rows = jnp.concatenate([msg[c * CAPS : (c + 1) * CAPS, :] for msg in messages], axis=0)
        total = own[c] + jnp.dot(picker, rows, preferred_element_type=F32)
        out[c] = total.astype(BF)


def gather(own, messages):
    return pl.pallas_call(
        gather_kernel,
        in_specs=[VMEM] * 5,
        out_specs=[VMEM] * 2,
        out_shape=[
            jax.ShapeDtypeStruct((3, BOX, E), BF),
            jax.ShapeDtypeStruct((BOX, 4 * CAPS), BF),
        ],
        compiler_params=params(),
        cost_estimate=cost(2e8, 3.3e6),
        name="gather",
    )(own, *messages)


def apply_kernel(first, count, last, *refs):
    sign, refs = refs[0], refs[1:]
    windows, refs = refs[:count], refs[count:]
    ops, counts, refs = refs[:7], refs[7], refs[8:]
    if last:
        before, pick, own_out, picks, refs = refs[0], refs[1], refs[2], refs[3:7], refs[7:]
        total = refs[0]
        refs = refs[1:]
    else:
        total, refs = refs[0], refs[1:]
    win_v, op_v, count_v, win_sem, op_sem, count_sem = refs
    win_copies = [
        pltpu.make_async_copy(windows[b], win_v.at[b], win_sem.at[b]) for b in range(count)
    ]
    op_copies, at = [], 0
    for n, ref in enumerate(ops):
        size = ref.shape[0]
        op_copies.append(pltpu.make_async_copy(ref, op_v.at[pl.ds(at, size)], op_sem.at[n]))
        at += size
    count_copies = [
        pltpu.make_async_copy(
            counts.at[pl.ds((first + b) * REFL + half * 8, 8)],
            count_v.at[pl.ds(b * REFL + half * 8, 8)],
            count_sem.at[b * 2 + half],
        )
        for b in range(count)
        for half in range(2)
    ]
    win_copies[0].start()
    op_copies[0].start()
    count_copies[0].start()
    for copy in op_copies[1:] + count_copies[1:] + win_copies[1:]:
        copy.start()
    total[...] = before[...] if last else jnp.zeros_like(total)
    due = {0: 0, 2: 1, 3: 2, 4: 3, 5: 4, 6: 5, 7: 6}
    for b in range(count):
        win_copies[b].wait()
        window = jnp.concatenate([win_v[b, c] for c in range(3)], axis=0)
        for step in range(REFL // 2):
            if b == 0 and step in due:
                op_copies[due[step]].wait()
            if step % 4 == 0:
                count_copies[b * 2 + step // 4].wait()
            r = 2 * step
            operator = jnp.concatenate([op_v[r], op_v[r + 1]], axis=1)
            moved = jnp.dot(window, operator, preferred_element_type=F32)
            rows = []
            for u in range(2):
                rows.append(
                    jnp.concatenate(
                        [
                            (
                                sign[(r + u) * 3 + c]
                                * moved[c * BOX : (c + 1) * BOX, u * COLS : (u + 1) * COLS]
                            ).astype(BF)
                            for c in range(3)
                        ],
                        axis=1,
                    )
                )
            lhs = jnp.concatenate(
                [count_v[b * REFL + r], count_v[b * REFL + r + 1]], axis=1
            )
            total[...] += jnp.dot(
                lhs, jnp.concatenate(rows, axis=0), preferred_element_type=F32
            )
    if last:
        summed = total[...]
        for c in range(3):
            own_out[c] = summed[:, c * COLS : (c + 1) * COLS]
        picked = lax.dot_general(
            pick[...], summed.astype(BF), (((0,), (0,)), ((), ())), preferred_element_type=F32
        ).astype(BF)
        for m in range(4):
            picks[m][...] = picked[m * CAPS : (m + 1) * CAPS]


def apply(sign, windows, ops, counts, first, last=()):
    count = len(windows)
    total = jax.ShapeDtypeStruct((BOX, 3 * COLS), F32)
    picks = [jax.ShapeDtypeStruct((CAPS, 3 * COLS), BF)] * 4
    own = jax.ShapeDtypeStruct((3, BOX, COLS), F32)
    scratch = [
        pltpu.VMEM((count, 3, BOX, E), BF),
        pltpu.VMEM((REFL, E, COLS), BF),
        pltpu.VMEM((count * REFL, BOX, BOX), BF),
        pltpu.SemaphoreType.DMA((count,)),
        pltpu.SemaphoreType.DMA((7,)),
        pltpu.SemaphoreType.DMA((count * 2,)),
    ]
    if last:
        scratch = [pltpu.VMEM((BOX, 3 * COLS), F32)] + scratch

    def kernel(*refs):
        apply_kernel(first, count, bool(last), *refs)

    return pl.pallas_call(
        kernel,
        in_specs=[SMEM] + [ANY] * (count + 8) + [VMEM] * len(last),
        out_specs=[VMEM] * 5 if last else VMEM,
        out_shape=[own] + picks if last else total,
        scratch_shapes=scratch,
        compiler_params=params(),
        cost_estimate=cost(count * 2.4e9, count * 3e6 + 2e6),
        name="apply_last" if last else "apply_first",
    )(sign, *windows, *ops, counts, *last)


def place_kernel(meta, *refs):
    out = refs[4]
    for m in range(4):
        rows = pl.ds(pl.multiple_of(meta[m] * CAPS, CAPS), CAPS)
        for c in range(3):
            out[c, rows, :] = refs[m][:, c * COLS : (c + 1) * COLS].astype(F32)


def place(meta, messages):
    return pl.pallas_call(
        place_kernel,
        in_specs=[SMEM] + [VMEM] * 4,
        out_specs=VMEM,
        out_shape=jax.ShapeDtypeStruct((3, 4 * CAPS, COLS), F32),
        compiler_params=params(),
        cost_estimate=cost(1e5, 6e5),
        name="place",
    )(meta, *messages)


def on_device(own_partial, spill_partial, spill_box, sources, reflections, operators):
    cube, pair = lax.axis_index("cube"), lax.axis_index("pair")
    count, pairs = lax.axis_size("cube"), lax.axis_size("pair")
    core, chip_odd = cube & 1, (cube >> 1) & 1
    chip = cube >> 1
    routes = neighbours(count)

    meta = jnp.stack([2 - core, 1 + core, 3 - 3 * chip_odd, 3 * chip_odd])
    offsets = jnp.array([-2, -1, 1, 2], jnp.int32)[:, None]
    there = (cube + offsets >= 0) & (cube + offsets < count)
    labels = jnp.where(there, spill_box.reshape(4, CAPS), -1).astype(F32)
    messages = pack(meta, spill_partial, jnp.tile(labels, (1, E // CAPS)))
    order = (1, 2, 3, 0)
    got = [None] * 4
    for m in order:
        got[m] = swapped(messages[m], routes[m], count)

    held = operators.shape[0]
    mine = lax.dynamic_slice(operators, (0, 0, COLS * pair), (held, E, COLS))
    direct = []
    for k in range(1, pairs):
        target = (pair - k) % pairs
        part = lax.dynamic_slice(operators, (2 * core, 0, COLS * target), (2, E, COLS))
        direct.append(
            lax.ppermute(part, "pair", [(s, (s - k) % pairs) for s in range(pairs)])
        )
    other = [swapped(part, routes[0], count) for part in direct]
    ops = [mine] + direct + other

    block = (sources >> 8) - cube
    block = jnp.where(block == 0, 0, jnp.where(block == 1 - 2 * core, 1, 2))
    k = ((reflections >> 2) - pair) & 3
    within = reflections & 3
    far = 2 * k + (within & 1) + jnp.where((within >> 1) == core, 2, 8)
    slot = jnp.where(k == 0, within, far)
    width = 256 - sources.shape[1]
    hi = jnp.pad((block * REFL + slot).astype(F32), ((0, 0), (0, width)), constant_values=-1)
    lo = jnp.pad((sources & 255).astype(F32), ((0, 0), (0, width)))
    slots = jnp.arange(REFL, dtype=jnp.int32)
    step = jnp.where(slots < 10, slots - 4, slots - 10)
    half = jnp.where(slots < 10, core, 1 - core)
    refl = 4 * ((pair + 1 + (step >> 1)) & 3) + 2 * half + (step & 1)
    refl = jnp.where(slots < 4, 4 * pair + slots, refl)
    bits = jnp.arange(3, dtype=jnp.int32)
    sign = (1 - 2 * ((refl[:, None] >> bits) & 1)).astype(F32).reshape(-1)

    steps = BOX // TB
    counts = table(hi, lo, 0, steps // 2)
    multipole, picker = gather(own_partial, got)
    across = swapped(multipole, routes[1], count)
    same = swapped(multipole, routes[0], count)
    hi, lo, _ = lax.optimization_barrier((hi, lo, multipole))
    counts = table(hi, lo, steps // 2, steps - steps // 2, counts)
    total = apply(sign, [multipole, same], ops, counts, 0)
    local_own, *picks = apply(sign, [across], ops, counts, 2, (total, picker))
    back = [None] * 4
    for m in order:
        back[m] = swapped(picks[m], routes[m], count)
    return local_own, place(meta, back)


def solution(mesh):
    in_specs = (
        P(None, "cube", None),
        P(None, "cube", None),
        P("cube"),
        P("cube", None),
        P("cube", None),
        P("pair", None, None),
    )
    out_specs = (P(None, "cube", "pair"), P(None, "cube", "pair"))
    return jax.shard_map(
        on_device, mesh=mesh, in_specs=in_specs, out_specs=out_specs, check_vma=False
    )
```
